32 devices in a mesh: dp: 4 (over y, x), row: 2 (over core), col: 4 (over z).
Axes of the slice: x: 2, y: 2, z: 4, core: 2. Of those that a mesh axis runs over, the one named last changes fastest.
Arguments:
- hidden_in: bfloat16 [8192, 768], P(('dp', 'col'), 'row'), may hold values from -36 to 36
- enc_states: bfloat16 [2048, 768], P(('dp', 'col'), 'row'), may hold values from -8 to 8
- grad_out: bfloat16 [8192, 768], P(('dp', 'col'), 'row'), may hold values from -6 to 6
- lengths: int32 [4], P('dp'), may hold values from 1024 to 2048, as said below
- buckets: int32 [2048], replicated, may hold values from 0 to 31, as said below
- self_gain: float32 [768], P('row'), may hold values from 0.1 to 1.9
- q_self: bfloat16 [768, 768], P('col', 'row'), may hold values from -0.02734375 to 0.02734375
- k_self: bfloat16 [768, 768], P('col', 'row'), may hold values from -0.21875 to 0.21875
- v_self: bfloat16 [768, 768], P('col', 'row'), may hold values from -0.21875 to 0.21875
- o_self: bfloat16 [768, 768], P('row', 'col'), may hold values from -2.5 to 2.5
- rel_table: float32 [12, 32], P('row'), may hold values from -4 to 4
- cross_gain: float32 [768], P('row'), may hold values from 0.1 to 1.9
- q_cross: bfloat16 [768, 768], P('col', 'row'), may hold values from -0.02734375 to 0.02734375
- k_cross: bfloat16 [768, 768], P('col', 'row'), may hold values from -0.21875 to 0.21875
- v_cross: bfloat16 [768, 768], P('col', 'row'), may hold values from -0.21875 to 0.21875
- o_cross: bfloat16 [768, 768], P('row', 'col'), may hold values from -2.5 to 2.5
- ff_gain: float32 [768], P('row'), may hold values from 0.1 to 1.9
- ff_gate: bfloat16 [768, 2048], P('col', 'row'), may hold values from -0.21875 to 0.21875
- ff_up: bfloat16 [768, 2048], P('col', 'row'), may hold values from -0.21875 to 0.21875
- ff_out: bfloat16 [2048, 768], P('row', 'col'), may hold values from -0.125 to 0.125
Outputs:
- out: bfloat16 [8192, 768], P(('dp', 'col'), 'row')
- grad_in: float32 [8192, 768], P(('dp', 'col'), 'row')
- grad_enc: float32 [2048, 768], P(('dp', 'col'), 'row')
- grad_self_gain: float32 [768], P('row')
- grad_q_self: float32 [768, 768], P('col', 'row')
- grad_k_self: float32 [768, 768], P('col', 'row')
- grad_v_self: float32 [768, 768], P('col', 'row')
- grad_o_self: float32 [768, 768], P('row', 'col')
- grad_rel_table: float32 [12, 32], P('row')
- grad_cross_gain: float32 [768], P('row')
- grad_q_cross: float32 [768, 768], P('col', 'row')
- grad_k_cross: float32 [768, 768], P('col', 'row')
- grad_v_cross: float32 [768, 768], P('col', 'row')
- grad_o_cross: float32 [768, 768], P('row', 'col')
- grad_ff_gain: float32 [768], P('row')
- grad_ff_gate: float32 [768, 2048], P('col', 'row')
- grad_ff_up: float32 [768, 2048], P('col', 'row')
- grad_ff_out: float32 [2048, 768], P('row', 'col')
The draws below stay inside these ranges and needn't reach their ends.
Inputs may be any that keep to these rules, and one draw needn't show every extreme that they name: `lengths`: some sequence has exactly 2048 valid tokens. Distance d has bucket d for d < 16; buckets never fall as the distance grows; distance 2048 - 1 has bucket 32 - 1.
All inputs are finite; a program needn't handle non-finite values.
Results may differ from the reference program's by a relative error of at most 0.025.
Values may be sent and summed in bfloat16 or wider, within the bound.
No kernel may reach another device: no remote copies, remote signals or barrier semaphores. Data moves between devices by JAX's collectives and lax.ppermute only.
A program may use at most 320 MiB of HBM per device.

```python
import jax
import jax.numpy as jnp
from jax import lax

D = 768
HEADS = 12
HS = 64
FF = 2048
NB = 32
HD = 768
LEN = 2048
ENC = 512
SEQS = 4
TOKENS = 8192
ENC_TOK = 2048


def draw_hidden_in(key, part):
    keys_split = jax.random.split(key, 1)
    base = jax.random.truncated_normal(keys_split[0], -4.0, 4.0, (TOKENS, D), jnp.float32)
    return base.astype(jnp.bfloat16)


def draw_enc_states(key, part):
    keys_split = jax.random.split(key, 1)
    base = jax.random.truncated_normal(keys_split[0], -4.0, 4.0, (ENC_TOK, D), jnp.float32)
    return base.astype(jnp.bfloat16)


def draw_rel_table(key, part):
    return jax.random.truncated_normal(key, -4.0, 4.0, (HEADS, NB), jnp.float32)


def draw_lengths(key, part):
    keys_split = jax.random.split(key, 2)
    drawn = jax.random.randint(keys_split[0], (SEQS,), LEN // 2, LEN + 1)
    chosen = jax.random.randint(keys_split[1], (), 0, SEQS)
    return jnp.where(jnp.arange(SEQS) == chosen, LEN, drawn).astype(jnp.int32)


def draw_buckets(key, part):
    breaks = jax.random.randint(key, (NB // 2 - 1,), NB // 2 + 1, LEN)
    distance = jnp.arange(LEN)
    passed = jnp.sum((distance[:, None] >= breaks[None, :]).astype(jnp.int32), axis=1)
    return jnp.where(distance < NB // 2, distance, NB // 2 + passed).astype(jnp.int32)


def block_levels(own_key, shape, cuts, least, top_value):
    factor_of = 1.0
    for axis_at, blocks in cuts:
        steps = jax.random.uniform(jax.random.fold_in(jax.random.fold_in(own_key, 6), axis_at), (blocks,), jnp.float32, least / len(cuts), top_value / len(cuts))
        factor_of = factor_of * jnp.repeat(jnp.exp(steps), shape[axis_at] // blocks).reshape((-1,) + (1,) * (len(shape) - 1 - axis_at))
    return factor_of


def noise(rng, shape, deviation, most, shards=(), dtype=jnp.bfloat16):
    array = jax.random.normal(rng, shape, jnp.float32) * deviation
    if len(shards) > 0:
        array = block_levels(rng, shape, shards, -0.22, 0.18) * array
    return jnp.clip(array, min=-most, max=most).astype(dtype)


def setup_inputs(seed: int = 0) -> dict:
    keys = jax.random.split(jax.random.key(seed), 21)
    hidden_in = draw_hidden_in(jax.random.fold_in(keys[20], 71), 0)
    enc_states = draw_enc_states(jax.random.fold_in(keys[20], 71), 0)
    grad_out = noise(keys[2], (TOKENS, D), 1.0, 6.0, ((0, 16), (1, 2)))
    lengths = draw_lengths(jax.random.fold_in(keys[20], 71), 0)
    buckets = draw_buckets(jax.random.fold_in(keys[20], 71), 0)
    self_gain = jnp.clip(1.0 + 0.18 * jax.random.normal(keys[5], (D,), jnp.float32), 0.1, 1.9)
    q_self = noise(keys[6], (D, HD), (D * HS) ** -0.5, 0.02734375, ((0, 4), (1, 2)))
    k_self = noise(keys[7], (D, HD), D ** -0.5, 0.21875, ((0, 4), (1, 2)))
    v_self = noise(keys[8], (D, HD), D ** -0.5, 0.21875, ((0, 4), (1, 2)))
    o_self = noise(keys[9], (HD, D), (max(HD // 128, 2)) ** -0.5, 2.5, ((0, 2), (1, 4)))
    rel_table = draw_rel_table(jax.random.fold_in(keys[20], 71), 0)
    cross_gain = jnp.clip(1.0 + 0.18 * jax.random.normal(keys[11], (D,), jnp.float32), 0.1, 1.9)
    q_cross = noise(keys[12], (D, HD), (D * HS) ** -0.5, 0.02734375, ((0, 4), (1, 2)))
    k_cross = noise(keys[13], (D, HD), D ** -0.5, 0.21875, ((0, 4), (1, 2)))
    v_cross = noise(keys[14], (D, HD), D ** -0.5, 0.21875, ((0, 4), (1, 2)))
    o_cross = noise(keys[15], (HD, D), (max(HD // 128, 2)) ** -0.5, 2.5, ((0, 2), (1, 4)))
    ff_gain = jnp.clip(1.0 + 0.18 * jax.random.normal(keys[16], (D,), jnp.float32), 0.1, 1.9)
    ff_gate = noise(keys[17], (D, FF), D ** -0.5, 0.21875, ((0, 4), (1, 2)))
    ff_up = noise(keys[18], (D, FF), D ** -0.5, 0.21875, ((0, 4), (1, 2)))
    ff_out = noise(keys[19], (FF, D), FF ** -0.5, 0.125, ((0, 2), (1, 4)))
    return {"hidden_in": hidden_in, "enc_states": enc_states, "grad_out": grad_out, "lengths": lengths, "buckets": buckets, "self_gain": self_gain, "q_self": q_self, "k_self": k_self, "v_self": v_self, "o_self": o_self, "rel_table": rel_table, "cross_gain": cross_gain, "q_cross": q_cross, "k_cross": k_cross, "v_cross": v_cross, "o_cross": o_cross, "ff_gain": ff_gain, "ff_gate": ff_gate, "ff_up": ff_up, "ff_out": ff_out}


EPSILON = 1e-06
NEGATIVE = -1e+30
GELU_SCALE = 0.7978845608028654

def matmul(left_side, right_side):
    return jnp.dot(left_side, right_side, preferred_element_type=jnp.float32)

def matmul_t(left_side, right_side):
    return jnp.dot(left_side, right_side.T, preferred_element_type=jnp.float32)

def tokens_t(left_side, right_side):
    return jnp.dot(left_side.T, right_side, preferred_element_type=jnp.float32)

def rounded(values):
    return lax.optimization_barrier(values.astype(jnp.bfloat16)).astype(jnp.float32)

def gelu_parts(gate_in):
    inner_arg = GELU_SCALE * (gate_in + 0.044715 * gate_in * gate_in * gate_in)
    tangent = jnp.tanh(inner_arg)
    gelu_value = 0.5 * gate_in * (1.0 + tangent)
    gelu_slope = 0.5 * (1.0 + tangent) + 0.5 * gate_in * (1.0 - tangent * tangent) * GELU_SCALE * (1.0 + 3.0 * 0.044715 * gate_in * gate_in)
    return (gelu_value, gelu_slope)

def rms_forward(values, gain_vec):
    scales = lax.rsqrt(lax.optimization_barrier(jnp.mean(values * values, axis=1, keepdims=True)) + EPSILON)
    normed = values * scales
    return (normed, scales, (normed * gain_vec).astype(jnp.bfloat16))

def rms_backward(upstream, normed, scales, gain_vec):
    scaled_grad = upstream * gain_vec
    average = lax.optimization_barrier(jnp.mean(scaled_grad * normed, axis=1, keepdims=True))
    return (scales * (scaled_grad - normed * average), lax.optimization_barrier(jnp.sum(upstream * normed, axis=0)))

def split_heads(values):
    return values.astype(jnp.float32).reshape(values.shape[0], HEADS, HS)

def attend(queries, key_mat, value_mat, bias, allowed):
    scores = jnp.einsum('qhd,khd->hqk', split_heads(queries), split_heads(key_mat))
    if bias is not None:
        scores = scores + bias
    if allowed is not None:
        scores = jnp.where(allowed[None], scores, NEGATIVE)
    row_peak = lax.optimization_barrier(jnp.max(scores, axis=2, keepdims=True))
    log_total = row_peak + jnp.log(lax.optimization_barrier(jnp.sum(jnp.exp(scores - row_peak), axis=2, keepdims=True)))
    attn_probs = jnp.exp(scores - log_total)
    context = jnp.einsum('hqk,khd->qhd', rounded(attn_probs), split_heads(value_mat))
    return (attn_probs, context.reshape(queries.shape[0], HD).astype(jnp.bfloat16))

def attend_back(queries, key_mat, value_mat, attn_probs, context, grad_context):
    grad_heads = split_heads(grad_context)
    grad_prob = jnp.einsum('qhd,khd->hqk', grad_heads, split_heads(value_mat))
    row_delta = jnp.einsum('qhd,qhd->hq', grad_heads, split_heads(context))
    dscore = attn_probs * (grad_prob - row_delta[:, :, None])
    dscore_b = rounded(dscore)
    grad_values = jnp.einsum('hqk,qhd->khd', rounded(attn_probs), grad_heads).reshape(-1, HD)
    grad_keys = jnp.einsum('hqk,qhd->khd', dscore_b, split_heads(queries)).reshape(-1, HD)
    grad_queries = jnp.einsum('hqk,khd->qhd', dscore_b, split_heads(key_mat)).reshape(-1, HD)
    return (grad_queries, grad_keys, grad_values, dscore)

def reference(hidden_in, enc_states, grad_out, lengths, buckets, self_gain, q_self, k_self, v_self, o_self, rel_table, cross_gain, q_cross, k_cross, v_cross, o_cross, ff_gain, ff_gate, ff_up, ff_out):
    positions = jnp.arange(LEN)
    distance_grid = jnp.clip(positions[:, None] - positions[None, :], 0, LEN - 1)
    bucket_grid = buckets[distance_grid]
    causal_grid = positions[None, :] <= positions[:, None]

    def bias_of(table_in):
        return table_in[:, bucket_grid]
    bias, table_pull = jax.vjp(bias_of, rel_table)
    w_qkv = jnp.concatenate([q_self, k_self, v_self], axis=1)
    w_ckv = jnp.concatenate([k_cross, v_cross], axis=1)
    w_ff = jnp.concatenate([ff_gate, ff_up], axis=1)

    def one_sequence(totals, inputs):
        hidden, encoder, upstream_b, length = inputs
        residual = hidden.astype(jnp.float32)
        allowed = causal_grid & (positions[None, :] < length)
        normed1, scales1, input1 = rms_forward(residual, self_gain)
        qkv = matmul(input1, w_qkv).astype(jnp.bfloat16)
        self_queries = qkv[:, :HD]
        self_keys = qkv[:, HD:2 * HD]
        self_values = qkv[:, 2 * HD:]
        self_probs, context = attend(self_queries, self_keys, self_values, bias, allowed)
        after_self = residual + matmul(context, o_self)
        normed2, scales2, input2 = rms_forward(after_self, cross_gain)
        cross_q = matmul(input2, q_cross).astype(jnp.bfloat16)
        cross_kv = matmul(encoder, w_ckv).astype(jnp.bfloat16)
        cross_keys = cross_kv[:, :HD]
        cross_values = cross_kv[:, HD:]
        cross_probs, cross_ctx = attend(cross_q, cross_keys, cross_values, None, None)
        after_cross = after_self + matmul(cross_ctx, o_cross)
        normed3, scales3, input3 = rms_forward(after_cross, ff_gain)
        gate_up = matmul(input3, w_ff)
        gate_part = gate_up[:, :FF]
        up_part = gate_up[:, FF:]
        activated, gelu_slope = gelu_parts(gate_part)
        hidden_units = (activated * up_part).astype(jnp.bfloat16)
        output = (after_cross + matmul(hidden_units, ff_out)).astype(jnp.bfloat16)
        upstream = upstream_b.astype(jnp.float32)
        grad_hidden = matmul_t(upstream_b, ff_out)
        grad_ff_out = tokens_t(hidden_units, upstream_b)
        grad_gate_up = jnp.concatenate([grad_hidden * up_part * gelu_slope, grad_hidden * activated], axis=1).astype(jnp.bfloat16)
        grad_input3 = matmul_t(grad_gate_up, w_ff)
        grad_w_ff = tokens_t(input3, grad_gate_up)
        grad_part3, grad_ff_gain = rms_backward(grad_input3, normed3, scales3, ff_gain)
        grad_after_cross = upstream + grad_part3
        down_cross = grad_after_cross.astype(jnp.bfloat16)
        grad_cross_ctx = matmul_t(down_cross, o_cross).astype(jnp.bfloat16)
        grad_o_cross = tokens_t(cross_ctx, down_cross)
        grad_cq, grad_ck, grad_cv, unused_cross = attend_back(cross_q, cross_keys, cross_values, cross_probs, cross_ctx, grad_cross_ctx)
        grad_cq_b = grad_cq.astype(jnp.bfloat16)
        grad_ckv = jnp.concatenate([grad_ck, grad_cv], axis=1).astype(jnp.bfloat16)
        grad_input2 = matmul_t(grad_cq_b, q_cross)
        grad_q_cross = tokens_t(input2, grad_cq_b)
        grad_encoder = matmul_t(grad_ckv, w_ckv)
        grad_w_ckv = tokens_t(encoder, grad_ckv)
        grad_part2, grad_cross_gain = rms_backward(grad_input2, normed2, scales2, cross_gain)
        grad_after_self = grad_after_cross + grad_part2
        down_self = grad_after_self.astype(jnp.bfloat16)
        grad_context = matmul_t(down_self, o_self).astype(jnp.bfloat16)
        grad_o_self = tokens_t(context, down_self)
        grad_q, grad_k, grad_v, dscore = attend_back(self_queries, self_keys, self_values, self_probs, context, grad_context)
        grad_table = table_pull(dscore)[0]
        grad_qkv = jnp.concatenate([grad_q, grad_k, grad_v], axis=1).astype(jnp.bfloat16)
        grad_input1 = matmul_t(grad_qkv, w_qkv)
        grad_w_qkv = tokens_t(input1, grad_qkv)
        grad_part1, grad_self_gain = rms_backward(grad_input1, normed1, scales1, self_gain)
        grad_input = grad_after_self + grad_part1
        found = (grad_self_gain, grad_w_qkv, grad_o_self, grad_table, grad_cross_gain, grad_q_cross, grad_w_ckv, grad_o_cross, grad_ff_gain, grad_w_ff, grad_ff_out)
        summed = tuple((total_now + found_now for total_now, found_now in zip(totals, found)))
        return (summed, (output, grad_input, grad_encoder))
    zeros_init = (jnp.zeros((D,), jnp.float32), jnp.zeros((D, 3 * HD), jnp.float32), jnp.zeros((HD, D), jnp.float32), jnp.zeros((HEADS, NB), jnp.float32), jnp.zeros((D,), jnp.float32), jnp.zeros((D, HD), jnp.float32), jnp.zeros((D, 2 * HD), jnp.float32), jnp.zeros((HD, D), jnp.float32), jnp.zeros((D,), jnp.float32), jnp.zeros((D, 2 * FF), jnp.float32), jnp.zeros((FF, D), jnp.float32))
    sequence_inputs = (hidden_in.reshape(SEQS, LEN, D), enc_states.reshape(SEQS, ENC, D), grad_out.reshape(SEQS, LEN, D), lengths)
    totals, (output, grad_input, grad_encoder) = lax.scan(one_sequence, zeros_init, sequence_inputs)
    g_self_gain, g_qkv, g_o_self, g_table, g_cross_gain, g_q_cross, g_ckv, g_o_cross, g_ff_gain, g_ff, g_ff_out = totals
    return (output.reshape(TOKENS, D), grad_input.reshape(TOKENS, D), grad_encoder.reshape(ENC_TOK, D), g_self_gain, g_qkv[:, :HD], g_qkv[:, HD:2 * HD], g_qkv[:, 2 * HD:], g_o_self, g_table, g_cross_gain, g_q_cross, g_ckv[:, :HD], g_ckv[:, HD:], g_o_cross, g_ff_gain, g_ff[:, :FF], g_ff[:, FF:], g_ff_out)
```

```python
from functools import partial

import jax
import jax.numpy as jnp
from jax import lax
from jax.experimental import pallas as pl
from jax.experimental.pallas import tpu as pltpu
from jax.sharding import PartitionSpec as P

HS = 64
PAIR = 128
EPSILON = 1e-06
NEGATIVE = -1e30
GELU_SCALE = 0.7978845608028654
BF = jnp.bfloat16
F32 = jnp.float32


def matmul(left_side, right_side):
    return jnp.dot(left_side, right_side, preferred_element_type=F32)


def matmul_t(left_side, right_side):
    return lax.dot_general(
        left_side, right_side, (((1,), (1,)), ((), ())), preferred_element_type=F32
    )


def tokens_t(left_side, right_side):
    return lax.dot_general(
        left_side, right_side, (((0,), (0,)), ((), ())), preferred_element_type=F32
    )


def gelu_parts(gate_in):
    inner_arg = GELU_SCALE * (gate_in + 0.044715 * gate_in * gate_in * gate_in)
    tangent = jnp.tanh(inner_arg)
    gelu_value = 0.5 * gate_in * (1.0 + tangent)
    gelu_slope = 0.5 * (1.0 + tangent) + 0.5 * gate_in * (1.0 - tangent * tangent) * GELU_SCALE * (
        1.0 + 3.0 * 0.044715 * gate_in * gate_in
    )
    return (gelu_value, gelu_slope)


def norm_forward(hidden, gain_vec):
    scales = lax.rsqrt(jnp.mean(hidden * hidden, axis=1, keepdims=True) + EPSILON)
    normed = hidden * scales
    return (normed, scales, (normed * gain_vec).astype(BF))


def norm_backward(upstream, normed, scales, gain_vec):
    scaled_grad = upstream * gain_vec
    average = jnp.mean(scaled_grad * normed, axis=1, keepdims=True)
    return scales * (scaled_grad - normed * average)


def table_kernel(line_ref, out_ref):
    wide = jnp.broadcast_to(line_ref[0], out_ref.shape[1:])
    out_ref[0] = pltpu.roll(wide, 0, 1, stride=1, stride_axis=0)


def build_tables(lines):
    head_count, _, width = lines.shape
    return pl.pallas_call(
        table_kernel,
        grid=(head_count,),
        in_specs=[pl.BlockSpec((1, 1, width), lambda h: (h, 0, 0))],
        out_specs=pl.BlockSpec((1, PAIR, width), lambda h: (h, 0, 0)),
        out_shape=jax.ShapeDtypeStruct((head_count, PAIR, width), F32),
        name="bias_tables",
    )(lines)


def diagonal_sums(spread):
    row_total = spread.shape[0]
    width = spread.shape[1]
    while row_total > 1:
        half = row_total // 2
        spread = spread[:half] + pltpu.roll(spread[half:], width - half, 1)
        row_total = half
        if row_total == 8:
            break
    total = spread[0:1]
    for step in range(1, 8):
        total = total + pltpu.roll(spread, width - step, 1)[step : step + 1]
    return total


def lane_pick(first_half, second_half):
    lanes = lax.broadcasted_iota(jnp.int32, first_half.shape, 1)
    return jnp.where(lanes < HS, first_half, second_half)


def head_only(values, slot):
    lanes = lax.broadcasted_iota(jnp.int32, values.shape, 1)
    keep = (lanes < HS) if slot == 0 else (lanes >= HS)
    return jnp.where(keep, values, jnp.zeros_like(values))


def forward_kernel(*refs, tile_k, biased, origin):
    if biased:
        (start_ref, q_ref, k_ref, v_ref, table_ref, pen_ref, out_ref, lse_ref) = refs
    else:
        (start_ref, q_ref, k_ref, v_ref, out_ref, lse_ref) = refs
    row_total = q_ref.shape[0]
    queries = q_ref[...]
    masked = [head_only(queries, slot) for slot in range(2)]
    first_row = start_ref[0]
    key_blocks = start_ref[1]

    def step(block, carry):
        begin = pl.multiple_of(block * tile_k, tile_k)
        keys = k_ref[pl.ds(begin, tile_k), :]
        vals = v_ref[pl.ds(begin, tile_k), :]
        fresh = []
        for slot in range(2):
            peak, total, acc = carry[slot]
            scores = matmul_t(masked[slot], keys)
            if biased:
                pieces = []
                for group in range(row_total // PAIR):
                    at = pl.multiple_of(begin - first_row - group * PAIR + origin, PAIR)
                    pieces.append(table_ref[slot, :, pl.ds(at, tile_k)])
                scores = scores + jnp.concatenate(pieces, axis=0) + pen_ref[:, pl.ds(begin, tile_k)]
            new_peak = jnp.maximum(peak, jnp.max(scores, axis=1, keepdims=True))
            decay = jnp.exp(peak - new_peak)
            probs = jnp.exp(scores - new_peak)
            total = total * decay + jnp.sum(probs, axis=1, keepdims=True)
            acc = acc * decay + matmul(probs.astype(BF), vals)
            fresh.append((new_peak, total, acc))
        return tuple(fresh)

    begin_state = tuple(
        (
            jnp.full((row_total, 1), -1e38, F32),
            jnp.zeros((row_total, 1), F32),
            jnp.zeros((row_total, PAIR), F32),
        )
        for _ in range(2)
    )
    done = lax.fori_loop(0, key_blocks, step, begin_state)
    (peak0, total0, acc0), (peak1, total1, acc1) = done
    out_ref[...] = lane_pick(acc0 / total0, acc1 / total1).astype(BF)
    for slot, (peak, total, _) in enumerate(done):
        column = jnp.broadcast_to(peak + jnp.log(total), (row_total, PAIR))
        lse_ref[slot] = column.T[:8]


def attend_forward(queries, keys, values, scalars, tables, penalty, tile_k, origin):
    row_total, width = queries.shape
    key_total = keys.shape[0]
    pairs = width // PAIR
    biased = tables is not None
    in_specs = [
        pl.BlockSpec((row_total, PAIR), lambda p, s: (0, p)),
        pl.BlockSpec((key_total, PAIR), lambda p, s: (0, p)),
        pl.BlockSpec((key_total, PAIR), lambda p, s: (0, p)),
    ]
    operands = [queries, keys, values]
    if biased:
        in_specs.append(pl.BlockSpec((2, PAIR, tables.shape[2]), lambda p, s: (p, 0, 0)))
        in_specs.append(pl.BlockSpec((1, key_total), lambda p, s: (0, 0)))
        operands += [tables, penalty]
    return pl.pallas_call(
        partial(forward_kernel, tile_k=tile_k, biased=biased, origin=origin),
        grid_spec=pltpu.PrefetchScalarGridSpec(
            num_scalar_prefetch=1,
            grid=(pairs,),
            in_specs=in_specs,
            out_specs=[
                pl.BlockSpec((row_total, PAIR), lambda p, s: (0, p)),
                pl.BlockSpec((2, 8, row_total), lambda p, s: (p, 0, 0)),
            ],
        ),
        out_shape=[
            jax.ShapeDtypeStruct((row_total, width), BF),
            jax.ShapeDtypeStruct((2 * pairs, 8, row_total), F32),
        ],
        compiler_params=pltpu.CompilerParams(vmem_limit_bytes=48 * 1024 * 1024),
        name="self_forward" if biased else "cross_forward",
    )(scalars, *operands)


def backward_kernel(*refs, tile_k, biased, origin):
    if biased:
        (
            start_ref, q_ref, k_ref, v_ref, g_ref, c_ref, lse_ref, table_ref, pen_ref,
            dq_ref, dk_ref, dv_ref, diag_ref, spread_ref,
        ) = refs
    else:
        (start_ref, q_ref, k_ref, v_ref, g_ref, c_ref, lse_ref, dq_ref, dk_ref, dv_ref) = refs
    row_total = q_ref.shape[0]
    key_total = k_ref.shape[0]
    first_row = start_ref[0]
    key_blocks = start_ref[1]
    queries = [head_only(q_ref[...], slot) for slot in range(2)]
    grads = [head_only(g_ref[...], slot) for slot in range(2)]
    product = (g_ref[...].astype(F32) * c_ref[...].astype(F32)).T
    deltas = [
        jnp.sum(product[slot * HS : (slot + 1) * HS], axis=0, keepdims=True) for slot in range(2)
    ]
    sums = [lse_ref[slot, 0:1, :] for slot in range(2)]
    if biased:
        spread_ref[...] = jnp.zeros_like(spread_ref)

    def step(block, carry):
        begin = pl.multiple_of(block * tile_k, tile_k)
        keys = k_ref[pl.ds(begin, tile_k), :]
        vals = v_ref[pl.ds(begin, tile_k), :]
        grad_keys = jnp.zeros((tile_k, PAIR), F32)
        grad_vals = jnp.zeros((tile_k, PAIR), F32)
        fresh = []
        for slot in range(2):
            scores = matmul_t(keys, queries[slot])
            if biased:
                places = []
                pieces = []
                for group in range(tile_k // PAIR):
                    at = pl.multiple_of(first_row - begin - group * PAIR + origin, PAIR)
                    places.append(at)
                    pieces.append(table_ref[slot, :, pl.ds(at, row_total)])
                scores = scores + jnp.concatenate(pieces, axis=0) + pen_ref[pl.ds(begin, tile_k), 0:1]
            probs = jnp.exp(scores - sums[slot])
            grad_probs = matmul_t(vals, grads[slot])
            dscore = probs * (grad_probs - deltas[slot])
            if biased:
                for group, at in enumerate(places):
                    spread_ref[slot, :, pl.ds(at, row_total)] += dscore[
                        group * PAIR : (group + 1) * PAIR
                    ]
            dscore_b = dscore.astype(BF)
            grad_vals = grad_vals + matmul(probs.astype(BF), grads[slot])
            grad_keys = grad_keys + matmul(dscore_b, queries[slot])
            fresh.append(carry[slot] + tokens_t(dscore_b, keys))
        dk_ref[pl.ds(begin, tile_k), :] = grad_keys.astype(BF)
        dv_ref[pl.ds(begin, tile_k), :] = grad_vals.astype(BF)
        return tuple(fresh)

    zero = jnp.zeros((row_total, PAIR), F32)
    dq0, dq1 = lax.fori_loop(0, key_blocks, step, (zero, zero))
    dq_ref[...] = lane_pick(dq0, dq1).astype(BF)

    def clear(block, carry):
        begin = pl.multiple_of(block * tile_k, tile_k)
        dk_ref[pl.ds(begin, tile_k), :] = jnp.zeros((tile_k, PAIR), BF)
        dv_ref[pl.ds(begin, tile_k), :] = jnp.zeros((tile_k, PAIR), BF)
        return carry

    lax.fori_loop(key_blocks, key_total // tile_k, clear, 0)
    if biased:
        for slot in range(2):
            diag_ref[slot] = diagonal_sums(spread_ref[slot])


def attend_backward(
    queries, keys, values, grads, context, sums, scalars, tables, penalty, tile_k, origin
):
    row_total, width = queries.shape
    key_total = keys.shape[0]
    pairs = width // PAIR
    biased = tables is not None
    row_spec = pl.BlockSpec((row_total, PAIR), lambda p, s: (0, p))
    key_spec = pl.BlockSpec((key_total, PAIR), lambda p, s: (0, p))
    in_specs = [
        row_spec, key_spec, key_spec, row_spec, row_spec,
        pl.BlockSpec((2, 8, row_total), lambda p, s: (p, 0, 0)),
    ]
    operands = [queries, keys, values, grads, context, sums]
    out_specs = [row_spec, key_spec, key_spec]
    out_shape = [
        jax.ShapeDtypeStruct((row_total, width), BF),
        jax.ShapeDtypeStruct((key_total, width), BF),
        jax.ShapeDtypeStruct((key_total, width), BF),
    ]
    scratch = []
    if biased:
        span = tables.shape[2]
        in_specs.append(pl.BlockSpec((2, PAIR, span), lambda p, s: (p, 0, 0)))
        in_specs.append(pl.BlockSpec((key_total, 1), lambda p, s: (0, 0)))
        operands += [tables, penalty]
        out_specs.append(pl.BlockSpec((2, 1, span), lambda p, s: (p, 0, 0)))
        out_shape.append(jax.ShapeDtypeStruct((2 * pairs, 1, span), F32))
        scratch.append(pltpu.VMEM((2, PAIR, span), F32))
    return pl.pallas_call(
        partial(backward_kernel, tile_k=tile_k, biased=biased, origin=origin),
        grid_spec=pltpu.PrefetchScalarGridSpec(
            num_scalar_prefetch=1,
            grid=(pairs,),
            in_specs=in_specs,
            out_specs=out_specs,
            scratch_shapes=scratch,
        ),
        out_shape=out_shape,
        compiler_params=pltpu.CompilerParams(vmem_limit_bytes=56 * 1024 * 1024),
        name="self_backward" if biased else "cross_backward",
    )(scalars, *operands)


def swap(values):
    return lax.ppermute(values, "row", [(0, 1), (1, 0)])


def join_feats(own, other):
    lower = lax.axis_index("row") == 0
    return jnp.where(
        lower, jnp.concatenate([own, other], axis=1), jnp.concatenate([other, own], axis=1)
    )


def own_feats(values):
    half = values.shape[1] // 2
    return lax.dynamic_slice_in_dim(values, lax.axis_index("row") * half, half, axis=1)


def other_feats(values):
    half = values.shape[1] // 2
    return lax.dynamic_slice_in_dim(values, (1 - lax.axis_index("row")) * half, half, axis=1)


def gather_weights(packed):
    return lax.all_gather(packed, "col", axis=0, tiled=True)


def scatter_weights(grads):
    mine = lax.psum_scatter(grads, "col", scatter_dimension=0, tiled=True)
    return lax.psum(mine, "dp")


def per_device(
    hidden_in, enc_states, grad_out, lengths, buckets,
    self_gain, q_self, k_self, v_self, o_self, rel_table,
    cross_gain, q_cross, k_cross, v_cross, o_cross,
    ff_gain, ff_gate, ff_up, ff_out,
):
    row_total, half = hidden_in.shape
    enc_rows = enc_states.shape[0]
    seq_len = row_total * lax.axis_size("col")
    first_row = lax.axis_index("col") * row_total
    wide = q_self.shape[1]
    ff_cols = ff_gate.shape[1]
    valid = lengths[0]

    self_w = gather_weights(jnp.concatenate([q_self, k_self, v_self], axis=1))
    rest_w = gather_weights(
        jnp.concatenate([o_self.T, q_cross, o_cross.T, k_cross, v_cross], axis=1)
    )
    ff_w = gather_weights(jnp.concatenate([ff_gate, ff_up, ff_out.T], axis=1))
    w_qkv = self_w
    o_self_t = rest_w[:, :wide]
    w_cq = rest_w[:, wide : 2 * wide]
    o_cross_t = rest_w[:, 2 * wide : 3 * wide]
    w_ckv = rest_w[:, 3 * wide :]
    w_gu = ff_w[:, : 2 * ff_cols]
    ff_out_t = ff_w[:, 2 * ff_cols :]

    packed_in = jnp.concatenate([hidden_in, enc_states, grad_out], axis=0)
    whole_in = join_feats(packed_in, swap(packed_in))
    residual = whole_in[:row_total].astype(F32)
    enc_whole = whole_in[row_total : row_total + enc_rows]
    upstream_b = whole_in[row_total + enc_rows :]
    gains = jnp.stack([self_gain, cross_gain, ff_gain])
    gains = join_feats(gains, swap(gains))
    gain1, gain2, gain3 = gains[0:1], gains[1:2], gains[2:3]

    tile_f = min(512, row_total)
    tile_b = min(256, row_total)
    reach = max(row_total, tile_f)
    onehot = (buckets[:, None] == jnp.arange(rel_table.shape[1])[None, :]).astype(F32)
    bias_dist = jnp.dot(rel_table, onehot.T, precision=lax.Precision.HIGHEST)
    head_count = bias_dist.shape[0]
    back_dist = jnp.flip(bias_dist, axis=1)
    origin_f = seq_len - PAIR
    origin_b = max(row_total, tile_b) - PAIR
    never = lambda count: jnp.full((head_count, count), NEGATIVE, F32)
    line_f = jnp.concatenate(
        [back_dist[:, PAIR - 1 :], never(reach), back_dist[:, : PAIR - 1]], axis=1
    )
    pad_f = (-line_f.shape[1]) % PAIR
    line_f = jnp.concatenate(
        [back_dist[:, PAIR - 1 :], never(reach + pad_f), back_dist[:, : PAIR - 1]], axis=1
    )
    line_b = jnp.concatenate([never(origin_b), bias_dist, never(PAIR)], axis=1)
    tables_f = build_tables(line_f[:, None, :])
    tables_b = build_tables(line_b[:, None, :])
    penalty = jnp.where(jnp.arange(seq_len) < valid, 0.0, NEGATIVE).astype(F32)
    last_key = jnp.minimum(first_row + row_total, valid)
    scalars_f = jnp.stack([first_row, (last_key + tile_f - 1) // tile_f]).astype(jnp.int32)
    scalars_b = jnp.stack([first_row, (last_key + tile_b - 1) // tile_b]).astype(jnp.int32)

    normed1, scales1, input1 = norm_forward(residual, gain1)
    qkv = matmul(input1, w_qkv).astype(BF)
    kv_all = lax.all_gather(qkv[:, wide:], "col", axis=0, tiled=True)
    keys_s, vals_s = kv_all[:, :wide], kv_all[:, wide:]
    cross_own = matmul(enc_whole, w_ckv).astype(BF)
    ckv_all = lax.all_gather(cross_own, "col", axis=0, tiled=True)
    keys_c, vals_c = ckv_all[:, :wide], ckv_all[:, wide:]
    queries_s = qkv[:, :wide]
    context, sums_s = attend_forward(
        queries_s, keys_s, vals_s, scalars_f, tables_f, penalty[None, :], tile_f, origin_f
    )
    part = matmul_t(context, o_self_t)
    after_self = residual + (part + swap(part))

    normed2, scales2, input2 = norm_forward(after_self, gain2)
    queries_c = matmul(input2, w_cq).astype(BF)
    tile_cf = min(512, keys_c.shape[0])
    tile_cb = min(256, keys_c.shape[0])
    scalars_cf = jnp.array([0, keys_c.shape[0] // tile_cf], jnp.int32)
    scalars_cb = jnp.array([0, keys_c.shape[0] // tile_cb], jnp.int32)
    context_c, sums_c = attend_forward(
        queries_c, keys_c, vals_c, scalars_cf, None, None, tile_cf, 0
    )
    part = matmul_t(context_c, o_cross_t)
    after_cross = after_self + (part + swap(part))

    normed3, scales3, input3 = norm_forward(after_cross, gain3)
    gate_up = matmul(input3, w_gu)
    gate_part = gate_up[:, :ff_cols]
    up_part = gate_up[:, ff_cols:]
    activated, gelu_slope = gelu_parts(gate_part)
    hidden_units = (activated * up_part).astype(BF)
    grad_hidden = matmul(upstream_b, ff_out_t)
    grad_gate_up = jnp.concatenate(
        [grad_hidden * up_part * gelu_slope, grad_hidden * activated], axis=1
    ).astype(BF)
    part3 = matmul_t(grad_gate_up, w_gu)
    grad_input3 = part3 + swap(part3)
    part = matmul_t(hidden_units, ff_out_t)
    output = (own_feats(after_cross) + (own_feats(part) + swap(other_feats(part)))).astype(BF)
    grad_ff = jnp.concatenate(
        [tokens_t(input3, grad_gate_up).astype(BF), tokens_t(upstream_b, hidden_units).astype(BF)],
        axis=1,
    )
    sum_ff = scatter_weights(grad_ff)
    grad_ff_gain = own_feats(jnp.sum(grad_input3 * normed3, axis=0, keepdims=True))
    grad_after_cross = upstream_b.astype(F32) + norm_backward(
        grad_input3, normed3, scales3, gain3
    )

    down_cross = grad_after_cross.astype(BF)
    grad_context_c = matmul(down_cross, o_cross_t).astype(BF)
    grad_cq, grad_ck, grad_cv = attend_backward(
        queries_c, keys_c, vals_c, grad_context_c, context_c, sums_c,
        scalars_cb, None, None, tile_cb, 0,
    )
    grad_ckv = lax.psum_scatter(
        jnp.concatenate([grad_ck, grad_cv], axis=1), "col", scatter_dimension=0, tiled=True
    )
    part = matmul_t(grad_cq, w_cq)
    grad_input2 = part + swap(part)
    grad_cross_gain = own_feats(jnp.sum(grad_input2 * normed2, axis=0, keepdims=True))
    grad_after_self = grad_after_cross + norm_backward(grad_input2, normed2, scales2, gain2)
    part = matmul_t(grad_ckv, w_ckv)
    grad_encoder = own_feats(part) + swap(other_feats(part))

    down_self = grad_after_self.astype(BF)
    grad_context = matmul(down_self, o_self_t).astype(BF)
    grad_q, grad_k, grad_v, diag = attend_backward(
        queries_s, keys_s, vals_s, grad_context, context, sums_s,
        scalars_b, tables_b, penalty[:, None], tile_b, origin_b,
    )
    grad_kv = lax.psum_scatter(
        jnp.concatenate([grad_k, grad_v], axis=1), "col", scatter_dimension=0, tiled=True
    )
    grad_rest = jnp.concatenate(
        [
            tokens_t(down_self, context).astype(BF),
            tokens_t(input2, grad_cq).astype(BF),
            tokens_t(down_cross, context_c).astype(BF),
            tokens_t(enc_whole, grad_ckv).astype(BF),
        ],
        axis=1,
    )
    sum_rest = scatter_weights(grad_rest)
    grad_dist = diag[:, 0, origin_b : origin_b + seq_len]
    grad_table = jnp.dot(grad_dist, onehot, precision=lax.Precision.HIGHEST)
    grad_qkv = jnp.concatenate([grad_q, grad_kv], axis=1)
    part = matmul_t(grad_qkv, w_qkv)
    grad_input1 = part + swap(part)
    sum_qkv = scatter_weights(tokens_t(input1, grad_qkv).astype(BF))
    grad_self_gain = own_feats(jnp.sum(grad_input1 * normed1, axis=0, keepdims=True))
    grad_input = own_feats(
        grad_after_self + norm_backward(grad_input1, normed1, scales1, gain1)
    )
    small = lax.psum(
        (grad_self_gain[0], grad_cross_gain[0], grad_ff_gain[0], grad_table), ("dp", "col")
    )
    sum_qkv = sum_qkv.astype(F32)
    sum_rest = sum_rest.astype(F32)
    sum_ff = sum_ff.astype(F32)
    return (
        output,
        grad_input,
        grad_encoder,
        small[0],
        sum_qkv[:, :wide],
        sum_qkv[:, wide : 2 * wide],
        sum_qkv[:, 2 * wide :],
        sum_rest[:, :wide].T,
        small[3],
        small[1],
        sum_rest[:, wide : 2 * wide],
        sum_rest[:, 3 * wide : 4 * wide],
        sum_rest[:, 4 * wide :],
        sum_rest[:, 2 * wide : 3 * wide].T,
        small[2],
        sum_ff[:, :ff_cols],
        sum_ff[:, ff_cols : 2 * ff_cols],
        sum_ff[:, 2 * ff_cols :].T,
    )


def solution(mesh):
    tokens = P(("dp", "col"), "row")
    stored = P("col", "row")
    turned = P("row", "col")
    return jax.shard_map(
        per_device,
        mesh=mesh,
        in_specs=(
            tokens, tokens, tokens, P("dp"), P(),
            P("row"), stored, stored, stored, turned, P("row", None),
            P("row"), stored, stored, stored, turned,
            P("row"), stored, stored, turned,
        ),
        out_specs=(
            tokens, tokens, tokens,
            P("row"), stored, stored, stored, turned, P("row", None),
            P("row"), stored, stored, stored, turned,
            P("row"), stored, stored, turned,
        ),
        check_vma=False,
    )
```

```python
from functools import partial

import jax
import jax.numpy as jnp
from jax import lax
from jax.experimental import pallas as pl
from jax.experimental.pallas import tpu as pltpu
from jax.sharding import PartitionSpec as P

HS = 64
PAIR = 128
EPSILON = 1e-06
NEGATIVE = -1e30
GELU_SCALE = 0.7978845608028654
BF = jnp.bfloat16
F32 = jnp.float32


def matmul(left_side, right_side):
    return jnp.dot(left_side, right_side, preferred_element_type=F32)


def matmul_t(left_side, right_side):
    return lax.dot_general(
        left_side, right_side, (((1,), (1,)), ((), ())), preferred_element_type=F32
    )


def tokens_t(left_side, right_side):
    return lax.dot_general(
        left_side, right_side, (((0,), (0,)), ((), ())), preferred_element_type=F32
    )


def gelu_parts(gate_in):
    inner_arg = GELU_SCALE * (gate_in + 0.044715 * gate_in * gate_in * gate_in)
    tangent = jnp.tanh(inner_arg)
    gelu_value = 0.5 * gate_in * (1.0 + tangent)
    gelu_slope = 0.5 * (1.0 + tangent) + 0.5 * gate_in * (1.0 - tangent * tangent) * GELU_SCALE * (
        1.0 + 3.0 * 0.044715 * gate_in * gate_in
    )
    return (gelu_value, gelu_slope)


def norm_forward(hidden, gain_vec):
    scales = lax.rsqrt(jnp.mean(hidden * hidden, axis=1, keepdims=True) + EPSILON)
    normed = hidden * scales
    return (normed, scales, (normed * gain_vec).astype(BF))


def norm_backward(upstream, normed, scales, gain_vec):
    scaled_grad = upstream * gain_vec
    average = jnp.mean(scaled_grad * normed, axis=1, keepdims=True)
    return scales * (scaled_grad - normed * average)


def table_kernel(line_ref, out_ref):
    wide = jnp.broadcast_to(line_ref[0], out_ref.shape[1:])
    out_ref[0] = pltpu.roll(wide, 0, 1, stride=1, stride_axis=0)


def build_tables(lines):
    head_count, _, width = lines.shape
    return pl.pallas_call(
        table_kernel,
        grid=(head_count,),
        in_specs=[pl.BlockSpec((1, 1, width), lambda h: (h, 0, 0))],
        out_specs=pl.BlockSpec((1, PAIR, width), lambda h: (h, 0, 0)),
        out_shape=jax.ShapeDtypeStruct((head_count, PAIR, width), F32),
        name="bias_tables",
    )(lines)


def diagonal_sums(spread):
    row_total = spread.shape[0]
    width = spread.shape[1]
    while row_total > 1:
        half = row_total // 2
        spread = spread[:half] + pltpu.roll(spread[half:], width - half, 1)
        row_total = half
        if row_total == 8:
            break
    total = spread[0:1]
    for step in range(1, 8):
        total = total + pltpu.roll(spread, width - step, 1)[step : step + 1]
    return total


def lane_pick(first_half, second_half):
    lanes = lax.broadcasted_iota(jnp.int32, first_half.shape, 1)
    return jnp.where(lanes < HS, first_half, second_half)


def head_only(values, slot):
    lanes = lax.broadcasted_iota(jnp.int32, values.shape, 1)
    keep = (lanes < HS) if slot == 0 else (lanes >= HS)
    return jnp.where(keep, values, jnp.zeros_like(values))


def forward_kernel(*refs, tile_k, biased, origin):
    if biased:
        (start_ref, q_ref, k_ref, v_ref, table_ref, pen_ref, out_ref, lse_ref) = refs
    else:
        (start_ref, q_ref, k_ref, v_ref, out_ref, lse_ref) = refs
    row_total = q_ref.shape[0]
    queries = q_ref[...]
    masked = [head_only(queries, slot) for slot in range(2)]
    key_blocks = start_ref[0]

    def step(block, carry):
        begin = pl.multiple_of(block * tile_k, tile_k)
        keys = k_ref[pl.ds(begin, tile_k), :]
        vals = v_ref[pl.ds(begin, tile_k), :]
        fresh = []
        for slot in range(2):
            peak, total, acc = carry[slot]
            scores = matmul_t(masked[slot], keys)
            if biased:
                pieces = []
                offset = begin - 2 * row_total * lax.div(begin, row_total) + origin
                for group in range(row_total // PAIR):
                    at = pl.multiple_of(offset - group * PAIR, PAIR)
                    pieces.append(table_ref[slot, :, pl.ds(at, tile_k)])
                scores = scores + jnp.concatenate(pieces, axis=0) + pen_ref[:, pl.ds(begin, tile_k)]
            new_peak = jnp.maximum(peak, jnp.max(scores, axis=1, keepdims=True))
            decay = jnp.exp(peak - new_peak)
            probs = jnp.exp(scores - new_peak)
            total = total * decay + jnp.sum(probs, axis=1, keepdims=True)
            acc = acc * decay + matmul(probs.astype(BF), vals)
            fresh.append((new_peak, total, acc))
        return tuple(fresh)

    begin_state = tuple(
        (
            jnp.full((row_total, 1), -1e38, F32),
            jnp.zeros((row_total, 1), F32),
            jnp.zeros((row_total, PAIR), F32),
        )
        for _ in range(2)
    )
    done = lax.fori_loop(0, key_blocks, step, begin_state)
    (peak0, total0, acc0), (peak1, total1, acc1) = done
    out_ref[...] = lane_pick(acc0 / total0, acc1 / total1).astype(BF)
    for slot, (peak, total, _) in enumerate(done):
        column = jnp.broadcast_to(peak + jnp.log(total), (row_total, PAIR))
        lse_ref[slot] = column.T[:8]


def attend_forward(queries, keys, values, scalars, tables, penalty, tile_k, origin):
    row_total, width = queries.shape
    key_total = keys.shape[0]
    pairs = width // PAIR
    biased = tables is not None
    in_specs = [
        pl.BlockSpec((row_total, PAIR), lambda p, s: (0, p)),
        pl.BlockSpec((key_total, PAIR), lambda p, s: (0, p)),
        pl.BlockSpec((key_total, PAIR), lambda p, s: (0, p)),
    ]
    operands = [queries, keys, values]
    if biased:
        in_specs.append(pl.BlockSpec((2, PAIR, tables.shape[2]), lambda p, s: (p, 0, 0)))
        in_specs.append(pl.BlockSpec((1, key_total), lambda p, s: (0, 0)))
        operands += [tables, penalty]
    return pl.pallas_call(
        partial(forward_kernel, tile_k=tile_k, biased=biased, origin=origin),
        grid_spec=pltpu.PrefetchScalarGridSpec(
            num_scalar_prefetch=1,
            grid=(pairs,),
            in_specs=in_specs,
            out_specs=[
                pl.BlockSpec((row_total, PAIR), lambda p, s: (0, p)),
                pl.BlockSpec((2, 8, row_total), lambda p, s: (p, 0, 0)),
            ],
        ),
        out_shape=[
            jax.ShapeDtypeStruct((row_total, width), BF),
            jax.ShapeDtypeStruct((2 * pairs, 8, row_total), F32),
        ],
        compiler_params=pltpu.CompilerParams(vmem_limit_bytes=48 * 1024 * 1024),
        name="self_forward" if biased else "cross_forward",
    )(scalars, *operands)


def backward_kernel(*refs, tile_k, biased, origin):
    if biased:
        (
            start_ref, q_ref, k_ref, v_ref, g_ref, c_ref, lse_ref, table_ref, pen_ref,
            dq_ref, dk_ref, dv_ref, diag_ref, spread_ref,
        ) = refs
    else:
        (start_ref, q_ref, k_ref, v_ref, g_ref, c_ref, lse_ref, dq_ref, dk_ref, dv_ref) = refs
    row_total = q_ref.shape[0]
    key_total = k_ref.shape[0]
    key_blocks = start_ref[0]
    queries = [head_only(q_ref[...], slot) for slot in range(2)]
    grads = [head_only(g_ref[...], slot) for slot in range(2)]
    product = (g_ref[...].astype(F32) * c_ref[...].astype(F32)).T
    deltas = [
        jnp.sum(product[slot * HS : (slot + 1) * HS], axis=0, keepdims=True) for slot in range(2)
    ]
    sums = [lse_ref[slot, 0:1, :] for slot in range(2)]
    if biased:
        spread_ref[...] = jnp.zeros_like(spread_ref)

    def step(block, carry):
        begin = pl.multiple_of(block * tile_k, tile_k)
        keys = k_ref[pl.ds(begin, tile_k), :]
        vals = v_ref[pl.ds(begin, tile_k), :]
        grad_keys = jnp.zeros((tile_k, PAIR), F32)
        grad_vals = jnp.zeros((tile_k, PAIR), F32)
        fresh = []
        for slot in range(2):
            scores = matmul_t(keys, queries[slot])
            if biased:
                places = []
                pieces = []
                offset = 2 * row_total * lax.div(begin, row_total) - begin + origin
                for group in range(tile_k // PAIR):
                    at = pl.multiple_of(offset - group * PAIR, PAIR)
                    places.append(at)
                    pieces.append(table_ref[slot, :, pl.ds(at, row_total)])
                scores = scores + jnp.concatenate(pieces, axis=0) + pen_ref[pl.ds(begin, tile_k), 0:1]
            probs = jnp.exp(scores - sums[slot])
            grad_probs = matmul_t(vals, grads[slot])
            dscore = probs * (grad_probs - deltas[slot])
            if biased:
                for group, at in enumerate(places):
                    spread_ref[slot, :, pl.ds(at, row_total)] += dscore[
                        group * PAIR : (group + 1) * PAIR
                    ]
            dscore_b = dscore.astype(BF)
            grad_vals = grad_vals + matmul(probs.astype(BF), grads[slot])
            grad_keys = grad_keys + matmul(dscore_b, queries[slot])
            fresh.append(carry[slot] + tokens_t(dscore_b, keys))
        dk_ref[pl.ds(begin, tile_k), :] = grad_keys.astype(BF)
        dv_ref[pl.ds(begin, tile_k), :] = grad_vals.astype(BF)
        return tuple(fresh)

    zero = jnp.zeros((row_total, PAIR), F32)
    dq0, dq1 = lax.fori_loop(0, key_blocks, step, (zero, zero))
    dq_ref[...] = lane_pick(dq0, dq1).astype(BF)

    def clear(block, carry):
        begin = pl.multiple_of(block * tile_k, tile_k)
        dk_ref[pl.ds(begin, tile_k), :] = jnp.zeros((tile_k, PAIR), BF)
        dv_ref[pl.ds(begin, tile_k), :] = jnp.zeros((tile_k, PAIR), BF)
        return carry

    lax.fori_loop(key_blocks, key_total // tile_k, clear, 0)
    if biased:
        for slot in range(2):
            diag_ref[slot] = diagonal_sums(spread_ref[slot])


def attend_backward(
    queries, keys, values, grads, context, sums, scalars, tables, penalty, tile_k, origin
):
    row_total, width = queries.shape
    key_total = keys.shape[0]
    pairs = width // PAIR
    biased = tables is not None
    row_spec = pl.BlockSpec((row_total, PAIR), lambda p, s: (0, p))
    key_spec = pl.BlockSpec((key_total, PAIR), lambda p, s: (0, p))
    in_specs = [
        row_spec, key_spec, key_spec, row_spec, row_spec,
        pl.BlockSpec((2, 8, row_total), lambda p, s: (p, 0, 0)),
    ]
    operands = [queries, keys, values, grads, context, sums]
    out_specs = [row_spec, key_spec, key_spec]
    out_shape = [
        jax.ShapeDtypeStruct((row_total, width), BF),
        jax.ShapeDtypeStruct((key_total, width), BF),
        jax.ShapeDtypeStruct((key_total, width), BF),
    ]
    scratch = []
    if biased:
        span = tables.shape[2]
        in_specs.append(pl.BlockSpec((2, PAIR, span), lambda p, s: (p, 0, 0)))
        in_specs.append(pl.BlockSpec((key_total, 1), lambda p, s: (0, 0)))
        operands += [tables, penalty]
        out_specs.append(pl.BlockSpec((2, 1, span), lambda p, s: (p, 0, 0)))
        out_shape.append(jax.ShapeDtypeStruct((2 * pairs, 1, span), F32))
        scratch.append(pltpu.VMEM((2, PAIR, span), F32))
    return pl.pallas_call(
        partial(backward_kernel, tile_k=tile_k, biased=biased, origin=origin),
        grid_spec=pltpu.PrefetchScalarGridSpec(
            num_scalar_prefetch=1,
            grid=(pairs,),
            in_specs=in_specs,
            out_specs=out_specs,
            scratch_shapes=scratch,
        ),
        out_shape=out_shape,
        compiler_params=pltpu.CompilerParams(vmem_limit_bytes=56 * 1024 * 1024),
        name="self_backward" if biased else "cross_backward",
    )(scalars, *operands)


def swap(values):
    return lax.ppermute(values, "row", [(0, 1), (1, 0)])


def join_feats(own, other):
    lower = lax.axis_index("row") == 0
    return jnp.where(
        lower, jnp.concatenate([own, other], axis=1), jnp.concatenate([other, own], axis=1)
    )


def own_feats(values):
    half = values.shape[1] // 2
    return lax.dynamic_slice_in_dim(values, lax.axis_index("row") * half, half, axis=1)


def other_feats(values):
    half = values.shape[1] // 2
    return lax.dynamic_slice_in_dim(values, (1 - lax.axis_index("row")) * half, half, axis=1)


def ring(axis, shift):
    count = lax.axis_size(axis)
    return [(i, (i + shift) % count) for i in range(count)]


def flip_bit(bit):
    return [(i, i ^ bit) for i in range(4)]


def line(axis, shift):
    count = lax.axis_size(axis)
    return [(i, i + shift) for i in range(count) if 0 <= i + shift < count]


def many_routes(row_total):
    count = lax.axis_size("dp")
    return count == 4 and row_total % (count * 16) == 0


def split_at(width):
    return (width // PAIR + 1) // 2 * PAIR


def place_kernel(*refs, block_rows, part_rows, cut, width, count):
    where_ref = refs[0]
    own_ref = refs[1]
    near = refs[2 : 2 + count - 1]
    left = refs[1 + count : 4 + count]
    right = refs[4 + count : 7 + count]
    out_ref = refs[7 + count]
    col = where_ref[0]
    spot = pl.multiple_of(col * block_rows, block_rows)
    out_ref[pl.ds(spot, block_rows), :] = own_ref[...]
    for step in range(1, count):
        base = lax.rem(col + count - step, count) * block_rows
        spot = pl.multiple_of(base + where_ref[1] * part_rows, part_rows)
        out_ref[pl.ds(spot, part_rows), :] = near[step - 1][...]
        rows = pl.ds((step - 1) * part_rows, part_rows)
        for bits in range(1, 4):
            spot = pl.multiple_of(base + where_ref[1 + bits] * part_rows, part_rows)
            out_ref[pl.ds(spot, part_rows), pl.ds(0, cut)] = left[bits - 1][rows, :]
            out_ref[pl.ds(spot, part_rows), pl.ds(cut, width - cut)] = right[bits - 1][rows, :]


def spread_dp(left, right):
    x_left = lax.ppermute(left, "dp", flip_bit(1))
    y_right = lax.ppermute(right, "dp", flip_bit(2))
    y_left = lax.ppermute(left, "dp", flip_bit(2))
    x_right = lax.ppermute(right, "dp", flip_bit(1))
    xy_left = lax.ppermute(x_left, "dp", flip_bit(2))
    xy_right = lax.ppermute(y_right, "dp", flip_bit(1))
    return (x_left, y_left, xy_left), (x_right, y_right, xy_right)


def gather_weights(packed):
    block_rows, width = packed.shape
    if not many_routes(block_rows):
        return lax.all_gather(packed, "col", axis=0, tiled=True)
    count = lax.axis_size("col")
    part_rows = block_rows // 4
    dp = lax.axis_index("dp")
    cut = split_at(width)
    part = lax.dynamic_slice_in_dim(packed, dp * part_rows, part_rows, axis=0)
    near = [lax.ppermute(part, "col", ring("col", step)) for step in range(1, count)]
    left = jnp.concatenate([piece[:, :cut] for piece in near], axis=0)
    right = jnp.concatenate([piece[:, cut:] for piece in near], axis=0)
    lefts, rights = spread_dp(left, right)
    where = jnp.stack([lax.axis_index("col"), dp, dp ^ 1, dp ^ 2, dp ^ 3]).astype(jnp.int32)
    return pl.pallas_call(
        partial(
            place_kernel, block_rows=block_rows, part_rows=part_rows, cut=cut, width=width,
            count=count,
        ),
        in_specs=[pl.BlockSpec(memory_space=pltpu.SMEM)]
        + [pl.BlockSpec(memory_space=pltpu.VMEM)] * (6 + count),
        out_specs=pl.BlockSpec(memory_space=pltpu.VMEM),
        out_shape=jax.ShapeDtypeStruct((count * block_rows, width), packed.dtype),
        name="place_weights",
    )(where, packed, *near, *lefts, *rights)


def add_rounded(first, second):
    return (first.astype(F32) + second.astype(F32)).astype(BF)


def pick(values, index, axis):
    return lax.dynamic_index_in_dim(values, index, axis, keepdims=False)


def unflip(values, axis, bit):
    return jnp.where(bit == 0, values, jnp.flip(values, axis))


def scatter_weights(grads):
    count = lax.axis_size("col")
    all_rows, width = grads.shape
    block_rows = all_rows // count
    if not many_routes(block_rows):
        mine = lax.psum_scatter(grads, "col", scatter_dimension=0, tiled=True)
        return lax.psum(mine, "dp").astype(F32)
    part_rows = block_rows // 4
    cut = split_at(width)
    dp = lax.axis_index("dp")
    col = lax.axis_index("col")
    x_bit, y_bit = dp % 2, dp // 2
    grid = grads.reshape(count, 2, 2, part_rows, width)
    left, right = grid[..., :cut], grid[..., cut:]
    got_left = lax.ppermute(pick(left, 1 - x_bit, 2), "dp", flip_bit(1))
    got_right = lax.ppermute(pick(right, 1 - y_bit, 1), "dp", flip_bit(2))
    left = add_rounded(pick(left, x_bit, 2), got_left)
    right = add_rounded(pick(right, y_bit, 1), got_right)
    got_left = lax.ppermute(pick(left, 1 - y_bit, 1), "dp", flip_bit(2))
    got_right = lax.ppermute(pick(right, 1 - x_bit, 1), "dp", flip_bit(1))
    left = add_rounded(pick(left, y_bit, 1), got_left)
    right = add_rounded(pick(right, x_bit, 1), got_right)
    blocks = jnp.concatenate([left, right], axis=2)
    total = pick(blocks, col, 0).astype(F32)
    for step in range(1, count):
        piece = pick(blocks, (col + step) % count, 0)
        total = total + lax.ppermute(piece, "col", ring("col", step)).astype(F32)
    total = total.astype(BF)
    (x_l, y_l, xy_l), (x_r, y_r, xy_r) = spread_dp(total[:, :cut], total[:, cut:])
    join = lambda one, two: jnp.concatenate([one, two], axis=1)
    parts = jnp.stack(
        [
            jnp.stack([total, join(x_l, x_r)]),
            jnp.stack([join(y_l, y_r), join(xy_l, xy_r)]),
        ]
    )
    parts = unflip(unflip(parts, 0, y_bit), 1, x_bit)
    return parts.reshape(block_rows, width).astype(F32)


def sum_small(values):
    for axis in ("dp", "col"):
        size = lax.axis_size(axis)
        bit = 1
        while bit < size:
            values = values + lax.ppermute(values, axis, [(i, i ^ bit) for i in range(size)])
            bit *= 2
    return values


def per_device(
    hidden_in, enc_states, grad_out, lengths, buckets,
    self_gain, q_self, k_self, v_self, o_self, rel_table,
    cross_gain, q_cross, k_cross, v_cross, o_cross,
    ff_gain, ff_gate, ff_up, ff_out,
):
    row_total, half = hidden_in.shape
    enc_rows = enc_states.shape[0]
    seq_len = row_total * lax.axis_size("col")
    first_row = lax.axis_index("col") * row_total
    wide = q_self.shape[1]
    ff_cols = ff_gate.shape[1]
    valid = lengths[0]

    self_w = gather_weights(jnp.concatenate([q_self, k_self, v_self], axis=1))
    rest_w = gather_weights(
        jnp.concatenate([o_self.T, q_cross, o_cross.T, k_cross, v_cross], axis=1)
    )
    ff_w = gather_weights(jnp.concatenate([ff_gate, ff_up, ff_out.T], axis=1))
    w_qkv = self_w
    o_self_t = rest_w[:, :wide]
    w_cq = rest_w[:, wide : 2 * wide]
    o_cross_t = rest_w[:, 2 * wide : 3 * wide]
    w_ckv = rest_w[:, 3 * wide :]
    w_gu = ff_w[:, : 2 * ff_cols]
    ff_out_t = ff_w[:, 2 * ff_cols :]

    col_count = lax.axis_size("col")
    behind = [hidden_in]
    for step in range(1, col_count):
        if step <= 2:
            behind.append(lax.ppermute(hidden_in, "col", line("col", step)))
        else:
            behind.append(lax.ppermute(behind[-1], "col", line("col", 1)))
    enc_all = [enc_states]
    for step in range(1, col_count):
        enc_all.append(lax.ppermute(enc_states, "col", ring("col", step)))
    first_in = jnp.concatenate([hidden_in, grad_out], axis=0)
    first_in = join_feats(first_in, swap(first_in))
    upstream_b = first_in[row_total:]
    whole_in = jnp.concatenate(
        [first_in[:row_total]] + [join_feats(piece, swap(piece)) for piece in behind[1:]], axis=0
    )
    enc_all = jnp.concatenate(enc_all, axis=0)
    enc_whole = join_feats(enc_all, swap(enc_all))
    residual_all = whole_in.astype(F32)
    residual = residual_all[:row_total]
    gains = jnp.stack([self_gain, cross_gain, ff_gain])
    gains = join_feats(gains, swap(gains))
    gain1, gain2, gain3 = gains[0:1], gains[1:2], gains[2:3]

    tile_f = min(512, row_total)
    tile_b = min(256, row_total)
    reach = max(row_total, tile_f)
    onehot = (buckets[:, None] == jnp.arange(rel_table.shape[1])[None, :]).astype(F32)
    bias_dist = jnp.dot(rel_table, onehot.T, precision=lax.Precision.HIGHEST)
    head_count = bias_dist.shape[0]
    back_dist = jnp.flip(bias_dist, axis=1)
    origin_f = seq_len - PAIR
    origin_b = max(row_total, tile_b) - PAIR
    never = lambda count: jnp.full((head_count, count), NEGATIVE, F32)
    line_f = jnp.concatenate(
        [back_dist[:, PAIR - 1 :], never(reach), back_dist[:, : PAIR - 1]], axis=1
    )
    pad_f = (-line_f.shape[1]) % PAIR
    line_f = jnp.concatenate(
        [back_dist[:, PAIR - 1 :], never(reach + pad_f), back_dist[:, : PAIR - 1]], axis=1
    )
    line_b = jnp.concatenate([never(origin_b), bias_dist, never(PAIR)], axis=1)
    tables_f = build_tables(line_f[:, None, :])
    tables_b = build_tables(line_b[:, None, :])
    place = jnp.arange(seq_len)
    position = first_row - place // row_total * row_total + place % row_total
    penalty = jnp.where((position >= 0) & (position < valid), 0.0, NEGATIVE).astype(F32)
    reached = first_row + row_total
    scalars_f = jnp.stack([reached // tile_f]).astype(jnp.int32)
    scalars_b = jnp.stack([reached // tile_b]).astype(jnp.int32)

    normed1, scales1, input1_all = norm_forward(residual_all, gain1)
    input1 = input1_all[:row_total]
    queries_s = matmul(input1, w_qkv[:, :wide]).astype(BF)
    kv_all = matmul(input1_all, w_qkv[:, wide:]).astype(BF)
    keys_s, vals_s = kv_all[:, :wide], kv_all[:, wide:]
    ckv_all = matmul(enc_whole, w_ckv).astype(BF)
    keys_c, vals_c = ckv_all[:, :wide], ckv_all[:, wide:]
    context, sums_s = attend_forward(
        queries_s, keys_s, vals_s, scalars_f, tables_f, penalty[None, :], tile_f, origin_f
    )
    part = matmul_t(context, o_self_t)
    after_self = residual + (part + swap(part))

    normed2, scales2, input2 = norm_forward(after_self, gain2)
    queries_c = matmul(input2, w_cq).astype(BF)
    tile_cf = min(512, keys_c.shape[0])
    tile_cb = min(256, keys_c.shape[0])
    scalars_cf = jnp.array([keys_c.shape[0] // tile_cf], jnp.int32)
    scalars_cb = jnp.array([keys_c.shape[0] // tile_cb], jnp.int32)
    context_c, sums_c = attend_forward(
        queries_c, keys_c, vals_c, scalars_cf, None, None, tile_cf, 0
    )
    part = matmul_t(context_c, o_cross_t)
    after_cross = after_self + (part + swap(part))

    normed3, scales3, input3 = norm_forward(after_cross, gain3)
    gate_up = matmul(input3, w_gu)
    gate_part = gate_up[:, :ff_cols]
    up_part = gate_up[:, ff_cols:]
    activated, gelu_slope = gelu_parts(gate_part)
    hidden_units = (activated * up_part).astype(BF)
    grad_hidden = matmul(upstream_b, ff_out_t)
    grad_gate_up = jnp.concatenate(
        [grad_hidden * up_part * gelu_slope, grad_hidden * activated], axis=1
    ).astype(BF)
    part3 = matmul_t(grad_gate_up, w_gu)
    grad_input3 = part3 + swap(part3)
    part = matmul_t(hidden_units, ff_out_t)
    output = (own_feats(after_cross) + (own_feats(part) + swap(other_feats(part)))).astype(BF)
    grad_ff = jnp.concatenate(
        [tokens_t(input3, grad_gate_up).astype(BF), tokens_t(upstream_b, hidden_units).astype(BF)],
        axis=1,
    )
    sum_ff = scatter_weights(grad_ff)
    grad_ff_gain = own_feats(jnp.sum(grad_input3 * normed3, axis=0, keepdims=True))
    grad_after_cross = upstream_b.astype(F32) + norm_backward(
        grad_input3, normed3, scales3, gain3
    )

    down_cross = grad_after_cross.astype(BF)
    grad_context_c = matmul(down_cross, o_cross_t).astype(BF)
    grad_cq, grad_ck, grad_cv = attend_backward(
        queries_c, keys_c, vals_c, grad_context_c, context_c, sums_c,
        scalars_cb, None, None, tile_cb, 0,
    )
    grad_ckv = jnp.concatenate([grad_ck, grad_cv], axis=1)
    part = matmul_t(grad_cq, w_cq)
    grad_input2 = part + swap(part)
    grad_cross_gain = own_feats(jnp.sum(grad_input2 * normed2, axis=0, keepdims=True))
    grad_after_self = grad_after_cross + norm_backward(grad_input2, normed2, scales2, gain2)
    part = matmul_t(grad_ckv, w_ckv)
    part = own_feats(part) + swap(other_feats(part).astype(BF)).astype(F32)
    grad_encoder = part[:enc_rows]
    for step in range(1, col_count):
        piece = part[step * enc_rows : (step + 1) * enc_rows].astype(BF)
        grad_encoder = grad_encoder + lax.ppermute(piece, "col", ring("col", -step)).astype(F32)

    down_self = grad_after_self.astype(BF)
    grad_context = matmul(down_self, o_self_t).astype(BF)
    grad_q, grad_k, grad_v, diag = attend_backward(
        queries_s, keys_s, vals_s, grad_context, context, sums_s,
        scalars_b, tables_b, penalty[:, None], tile_b, origin_b,
    )
    grad_kv = jnp.concatenate([grad_k, grad_v], axis=1)
    grad_rest = jnp.concatenate(
        [
            tokens_t(down_self, context).astype(BF),
            tokens_t(input2, grad_cq).astype(BF),
            tokens_t(down_cross, context_c).astype(BF),
            tokens_t(enc_whole, grad_ckv).astype(BF),
        ],
        axis=1,
    )
    sum_rest = scatter_weights(grad_rest)
    grad_dist = diag[:, 0, origin_b : origin_b + seq_len]
    grad_table = jnp.dot(grad_dist, onehot, precision=lax.Precision.HIGHEST)
    sum_qkv = scatter_weights(
        jnp.concatenate(
            [tokens_t(input1, grad_q).astype(BF), tokens_t(input1_all, grad_kv).astype(BF)], axis=1
        )
    )
    part = matmul_t(grad_kv, w_qkv[:, wide:])
    part = jnp.concatenate(
        [part[:row_total] + matmul_t(grad_q, w_qkv[:, :wide]), part[row_total:]], axis=0
    )
    part = own_feats(part) + swap(other_feats(part).astype(BF)).astype(F32)
    grad_self_gain = jnp.sum(part * own_feats(normed1), axis=0)
    grad_input1 = part[:row_total]
    for step in range(1, col_count):
        piece = part[step * row_total : (step + 1) * row_total].astype(BF)
        grad_input1 = grad_input1 + lax.ppermute(piece, "col", line("col", -step)).astype(F32)
    own_normed = own_feats(normed1[:row_total])
    scaled_grad = grad_input1 * self_gain[None, :]
    totals = jnp.sum(scaled_grad * own_normed, axis=1)
    average = ((totals + swap(totals)) / (2 * half))[:, None]
    grad_input = own_feats(grad_after_self) + scales1[:row_total] * (
        scaled_grad - own_normed * average
    )
    small = sum_small(
        jnp.concatenate(
            [grad_self_gain, grad_cross_gain[0], grad_ff_gain[0], grad_table.reshape(-1)]
        )
    )
    small = (
        small[:half],
        small[half : 2 * half],
        small[2 * half : 3 * half],
        small[3 * half :].reshape(grad_table.shape),
    )
    return (
        output,
        grad_input,
        grad_encoder,
        small[0],
        sum_qkv[:, :wide],
        sum_qkv[:, wide : 2 * wide],
        sum_qkv[:, 2 * wide :],
        sum_rest[:, :wide].T,
        small[3],
        small[1],
        sum_rest[:, wide : 2 * wide],
        sum_rest[:, 3 * wide : 4 * wide],
        sum_rest[:, 4 * wide :],
        sum_rest[:, 2 * wide : 3 * wide].T,
        small[2],
        sum_ff[:, :ff_cols],
        sum_ff[:, ff_cols : 2 * ff_cols],
        sum_ff[:, 2 * ff_cols :].T,
    )


def solution(mesh):
    tokens = P(("dp", "col"), "row")
    stored = P("col", "row")
    turned = P("row", "col")
    return jax.shard_map(
        per_device,
        mesh=mesh,
        in_specs=(
            tokens, tokens, tokens, P("dp"), P(),
            P("row"), stored, stored, stored, turned, P("row", None),
            P("row"), stored, stored, stored, turned,
            P("row"), stored, stored, turned,
        ),
        out_specs=(
            tokens, tokens, tokens,
            P("row"), stored, stored, stored, turned, P("row", None),
            P("row"), stored, stored, stored, turned,
            P("row"), stored, stored, turned,
        ),
        check_vma=False,
    )
```
